32 devices in a mesh: groups: 2 (over x), blk: 16 (over z, y, core).
Axes of the slice: x: 2, y: 2, z: 4, core: 2. Of those that a mesh axis runs over, the one named last changes fastest.
Arguments:
- text_queries: bfloat16 [4096, 4096], P(('groups', 'blk')), parts along dimension 0, may hold values from -170 to 170
- image_states: bfloat16 [1536, 8192], P(('groups', 'blk')), parts along dimension 0, may hold values from -6 to 6
- kv_weight: bfloat16 [8192, 1024], P('blk'), may hold values from -0.1875 to 0.1875
- q_gain: float32 [128], replicated, may hold values from 0.25 to 1.75
- k_gain: float32 [128], replicated, may hold values from 0.25 to 1.75
- text_counts: int32 [6], P('groups'), parts along dimension 0, may hold values from 1 to 1024, 2048 in all
- image_counts: int32 [6], P('groups'), parts along dimension 0, may hold values from 96 to 384, as said below
Outputs:
- attended: bfloat16 [4096, 4096], P(('groups', 'blk')), parts along dimension 0
The draws below stay inside these ranges and needn't reach their ends.
There are 2 independent parts, one for each index of `groups`. The reference program is written for one: setup_inputs(seed, part) draws one part's arguments, and reference() takes and returns one part's arrays. A program takes and returns all parts, laid end to end along the dimension named above; an argument that names none is the same for every part. Nothing has to cross between parts.
Inputs may be any that keep to these rules, and one draw needn't show every extreme that they name: `text_counts`: they sum to 2048. `image_counts`: they sum to 768; the second image has exactly 384 tokens, the first and last are cut by the window.
All inputs are finite; a program needn't handle non-finite values.
Results may differ from the reference program's by a relative error of at most 0.0071.
Values may be sent and summed in bfloat16 or wider, within the bound.
No kernel may reach another device: no remote copies, remote signals or barrier semaphores. Data moves between devices by JAX's collectives and lax.ppermute only.
A program may use at most 128 MiB of HBM per device.

```python
import math
import jax
import jax.numpy as jnp
import numpy as np
from jax import lax

D = 8192
HD = 128
QH = 32
KVH = 4
IMAGES = 3
TXT = 2048
IMG = 768


def draw_text_queries(key, part):
    key_base, key_column = jax.random.split(key, 2)
    base_values = jnp.clip(jax.random.normal(key_base, (TXT, QH * HD), jnp.float32), -4.0, 4.0)
    column_scale = jnp.exp(jax.random.uniform(key_column, (1, QH * HD), jnp.float32) * math.log(10.0))
    return (base_values * column_scale).astype(jnp.bfloat16)


def draw_image_counts(key, part):
    first = jax.random.randint(key, (), IMG // 8, 3 * IMG // 8 + 1, dtype=jnp.int32)
    middle = jnp.full((), IMG // 2, jnp.int32)
    last = IMG - IMG // 2 - first
    return jnp.stack([first, middle, last]).astype(jnp.int32)


def steps_of(key, extent, cuts, least, top_value):
    factor_of = 1.0
    for position, blocks in cuts:
        steps = jax.random.uniform(jax.random.fold_in(jax.random.fold_in(key, 6), position), (blocks,), jnp.float32, least / len(cuts), top_value / len(cuts))
        factor_of = factor_of * jnp.repeat(jnp.exp(steps), extent[position] // blocks).reshape((-1,) + (1,) * (len(extent) - 1 - position))
    return factor_of


def split_up(number_of, total, limit, lean):
    portions = [(1 << 20) // math.isqrt(grade ** lean) + 1 for grade in range(2, number_of + 1)]
    spare, counts = total - limit - (number_of - 1), [1] * (number_of - 1)
    while spare > 0:
        free = [i for i in range(number_of - 1) if counts[i] < limit]
        pool, budget = sum([portions[i] for i in free]), spare
        for i in free:
            extra = min(limit - counts[i], max(1, budget * portions[i] // pool), spare)
            counts[i] = counts[i] + extra
            spare = spare - extra
    return np.array([limit] + counts)


def ragged_sizes(own_key, number_of, total, limit, lean):
    if number_of == 2:
        one = jax.random.randint(own_key, (), max(1, total - limit), min(limit, total - 1) + 1)
        return jnp.stack([one, total - one])
    lengths = jnp.asarray(split_up(number_of, total, limit, lean), jnp.int32)
    pairs = (number_of - 1) // 2
    donor, taker = lengths[1:1 + 2 * pairs:2], lengths[2:2 + 2 * pairs:2]
    slack = jnp.minimum(donor - 1, limit - taker)
    moved = jax.random.randint(jax.random.fold_in(own_key, 1), (pairs,), 0, 1 << 20) % (slack + 1)
    lengths = lengths.at[1:1 + 2 * pairs:2].set(donor - moved).at[2:2 + 2 * pairs:2].set(taker + moved)
    return lengths[jax.random.permutation(jax.random.fold_in(own_key, 2), number_of)]


def noise(stream_key, shape, spread, reach, pieces=(), held_as=jnp.bfloat16):
    array = spread * jax.random.normal(stream_key, shape, jnp.float32)
    if pieces:
        array = array * steps_of(stream_key, shape, pieces, -0.22, 0.18)
    return jnp.clip(array, -reach, reach).astype(held_as)


def setup_inputs(seed: int = 0, part: int = 0) -> dict:
    seeds = jax.random.split(jax.random.key(seed), 8)
    part_splits = jax.random.split(jax.random.fold_in(seeds[7], part), 8)
    return {
        "text_queries": draw_text_queries(jax.random.fold_in(jax.random.fold_in(seeds[7], part), 71), part),
        "image_states": noise(part_splits[1], (IMG, D), 1.0, 6.0, ((0, 16),)),
        "kv_weight": noise(seeds[2], (D, 2 * KVH * HD), (D // 8) ** -0.5, 0.1875, ((0, 16),)),
        "q_gain": jnp.clip(1.0 + 0.15 * jax.random.normal(seeds[3], (HD,), jnp.float32), 0.25, 1.75),
        "k_gain": jnp.clip(1.0 + 0.15 * jax.random.normal(seeds[4], (HD,), jnp.float32), 0.25, 1.75),
        "text_counts": ragged_sizes(part_splits[5], IMAGES, TXT, TXT // 2, 2).astype(jnp.int32),
        "image_counts": draw_image_counts(jax.random.fold_in(jax.random.fold_in(seeds[7], part), 71), part),
    }


epsilon = 1e-05

def rms_norm(inputs, norm_gain):
    return inputs * lax.rsqrt(lax.optimization_barrier(jnp.mean(inputs * inputs, axis=-1, keepdims=True)) + epsilon) * norm_gain

def reference(text_queries, image_states, kv_weight, q_gain, k_gain, text_counts, image_counts):
    kv_width = KVH * HD
    group_size = QH // KVH
    projected = jnp.dot(image_states, kv_weight, preferred_element_type=jnp.float32)
    image_keys = rms_norm(projected[:, :kv_width].reshape(IMG, KVH, HD), k_gain).astype(jnp.bfloat16)
    image_values = projected[:, kv_width:].reshape(IMG, KVH, HD).astype(jnp.bfloat16)
    normed_queries = rms_norm(text_queries.astype(jnp.float32).reshape(TXT, QH, HD), q_gain).astype(jnp.bfloat16)
    normed_queries = normed_queries.reshape(TXT, KVH, group_size, HD)
    key_float = lax.optimization_barrier(image_keys).astype(jnp.float32)
    value_float = lax.optimization_barrier(image_values).astype(jnp.float32)
    query_float = lax.optimization_barrier(normed_queries).astype(jnp.float32)
    text_ends = jnp.cumsum(text_counts).astype(jnp.int32)
    image_ends = jnp.cumsum(image_counts).astype(jnp.int32)
    text_positions = jnp.arange(TXT, dtype=jnp.int32)
    image_positions = jnp.arange(IMG, dtype=jnp.int32)
    text_segment = lax.optimization_barrier(jnp.sum((text_ends[None, :] <= text_positions[:, None]).astype(jnp.int32), axis=1))
    image_owner = lax.optimization_barrier(jnp.sum((image_ends[None, :] <= image_positions[:, None]).astype(jnp.int32), axis=1))
    score_scale = 1.0 / math.sqrt(HD)
    row_block = math.gcd(TXT, 512)

    def attend_block(block_index):
        first_row = (block_index * row_block).astype(jnp.int32)
        query_rows = lax.dynamic_slice_in_dim(query_float, first_row, row_block, 0)
        segment = lax.dynamic_slice_in_dim(text_segment, first_row, row_block, 0)
        scores = jnp.einsum('tgrd,pgd->grtp', query_rows, key_float) * score_scale
        allowed = image_owner[None, :] <= segment[:, None]
        weights = jnp.where(allowed[None, None], jnp.exp(scores), 0.0)
        totals = lax.optimization_barrier(jnp.sum(weights, axis=-1))
        rounded = lax.optimization_barrier(weights.astype(jnp.bfloat16)).astype(jnp.float32)
        summed = jnp.einsum('grtp,pgd->tgrd', rounded, value_float)
        return (summed / jnp.transpose(totals, (2, 0, 1))[..., None]).astype(jnp.bfloat16)
    blocks = lax.map(attend_block, jnp.arange(TXT // row_block, dtype=jnp.int32))
    return blocks.reshape(TXT, QH * HD)
```

```python
import functools
import math

import jax
import jax.numpy as jnp
from jax import lax
from jax.experimental import pallas as pl
from jax.experimental.pallas import tpu as pltpu
from jax.sharding import PartitionSpec as P

epsilon = 1e-05
LANE = 4


def norm_kernel(heads, head_dim, x_ref, gain_ref, out_ref):
    gain = gain_ref[...]
    for h in range(heads):
        columns = slice(h * head_dim, (h + 1) * head_dim)
        x = x_ref[:, columns].astype(jnp.float32)
        scale = lax.rsqrt(jnp.mean(x * x, axis=-1, keepdims=True) + epsilon)
        out_ref[:, columns] = (x * scale * gain).astype(out_ref.dtype)


def norm_queries(queries, gain):
    rows, width = queries.shape
    head_dim = gain.shape[-1]
    return pl.pallas_call(
        functools.partial(norm_kernel, width // head_dim, head_dim),
        out_shape=jax.ShapeDtypeStruct((rows, width), jnp.bfloat16),
        name="norm_queries",
    )(queries, gain)


def attend_kernel(group_size, head_dim, n_sets, q_ref, segment_ref, bias_ref, *refs):
    kv_refs, out_ref = refs[:-1], refs[-1]
    k_refs, v_refs = kv_refs[:n_sets], kv_refs[n_sets:]
    rows = q_ref.shape[0]
    segment = segment_ref[...]
    keys = jnp.concatenate([r[...] for r in k_refs], axis=0)
    values = jnp.concatenate([r[...] for r in v_refs], axis=0)
    keys = jnp.concatenate([keys, bias_ref[...]], axis=1)
    values = jnp.concatenate([values, jnp.ones_like(values)], axis=1)
    stack = math.gcd(group_size, 4)
    for first in range(0, group_size, stack):
        spans = [slice(h * head_dim, (h + 1) * head_dim) for h in range(first, first + stack)]
        q = jnp.concatenate(
            [jnp.concatenate([q_ref[:, span], segment], axis=1) for span in spans], axis=0
        )
        scores = lax.dot_general(
            q, keys, (((1,), (1,)), ((), ())), preferred_element_type=jnp.float32
        )
        weights = jnp.exp2(scores).astype(jnp.bfloat16)
        sums = jnp.dot(weights, values, preferred_element_type=jnp.float32)
        result = (sums[:, :head_dim] / sums[:, head_dim:]).astype(out_ref.dtype)
        for i, span in enumerate(spans):
            out_ref[:, span] = result[i * rows : (i + 1) * rows]


def attend(queries, segment, bias, sets, head_dim):
    rows, width = queries.shape
    kv_heads = sets[0].shape[1] // (2 * head_dim)
    group_size = width // head_dim // kv_heads
    span = sets[0].shape[0]
    whole = lambda g: (0, 0)
    return pl.pallas_call(
        functools.partial(attend_kernel, group_size, head_dim, len(sets)),
        grid=(kv_heads,),
        in_specs=[
            pl.BlockSpec((rows, group_size * head_dim), lambda g: (0, g)),
            pl.BlockSpec(segment.shape, whole),
            pl.BlockSpec(bias.shape, whole),
            *[pl.BlockSpec((span, head_dim), lambda g: (0, g)) for _ in sets],
            *[pl.BlockSpec((span, head_dim), lambda g: (0, g + kv_heads)) for _ in sets],
        ],
        out_specs=pl.BlockSpec((rows, group_size * head_dim), lambda g: (0, g)),
        out_shape=jax.ShapeDtypeStruct((rows, width), jnp.bfloat16),
        name="attend",
    )(queries, segment, bias, *sets, *sets)


def body(n_blk, text_queries, image_states, kv_weight, q_gain, k_gain, text_counts, image_counts):
    head_dim = q_gain.shape[0]
    text_rows = text_queries.shape[0]
    image_rows = image_states.shape[0]
    kv_width = kv_weight.shape[1] // 2
    kv_heads = kv_width // head_dim
    depth = kv_weight.shape[0]
    images = text_counts.shape[0]
    planes = n_blk // LANE
    me = lax.axis_index("blk")
    plane, lane = me // LANE, me % LANE

    def swap_lane(x, bits):
        return lax.ppermute(x, "blk", [(i, i ^ bits) for i in range(n_blk)])

    def swap_plane(x, step):
        return lax.ppermute(x, "blk", [(i, i ^ (step * LANE)) for i in range(n_blk)])

    span = LANE * depth
    received = [lax.dynamic_slice_in_dim(image_states, plane * span, span, 1)]
    for step in range(1, planes):
        outgoing = lax.dynamic_slice_in_dim(image_states, (plane ^ step) * span, span, 1)
        received.append(swap_plane(outgoing, step))
    weights = [kv_weight, swap_lane(kv_weight, 1), swap_lane(kv_weight, 2)]
    weights.append(swap_lane(weights[2], 1))

    queries = norm_queries(text_queries, q_gain[None, :])
    positions = me * text_rows + jnp.arange(text_rows, dtype=jnp.int32)
    text_ends, image_ends = jnp.cumsum(text_counts), jnp.cumsum(image_counts)
    text_segment = jnp.sum((text_ends[None, :] <= positions[:, None]).astype(jnp.int32), axis=1)
    slots = -(-(images + 1) // 128) * 128
    slot = jnp.arange(slots, dtype=jnp.int32)
    segment = (text_segment[:, None] == slot[None, :]).astype(jnp.bfloat16)
    r = jnp.arange(image_rows, dtype=jnp.int32)[None, None, :]
    s = jnp.arange(planes, dtype=jnp.int32)[None, :, None]
    j = jnp.arange(LANE, dtype=jnp.int32)[:, None, None]
    image_positions = ((((plane ^ s) * LANE) + (lane ^ j)) * image_rows + r).reshape(-1)
    owner = jnp.sum((image_ends[None, :] <= image_positions[:, None]).astype(jnp.int32), axis=1)
    bias = jnp.where(owner[:, None] <= slot[None, :], 0.0, -30000.0).astype(jnp.bfloat16)
    received, queries, segment, bias = lax.optimization_barrier(
        (received, queries, segment, bias)
    )

    stacked = jnp.concatenate(received, axis=0)
    partial = jnp.zeros((planes * image_rows, 2 * kv_width), jnp.float32)
    for j in range(LANE):
        columns = lax.dynamic_slice_in_dim(stacked, (lane ^ j) * depth, depth, 1)
        partial = partial + jnp.dot(columns, weights[j], preferred_element_type=jnp.float32)
    projected = partial[:image_rows]
    for step in range(1, planes):
        outgoing = partial[step * image_rows : (step + 1) * image_rows].astype(jnp.bfloat16)
        projected = projected + swap_plane(outgoing, step).astype(jnp.float32)
    keys = projected[:, :kv_width].reshape(image_rows, kv_heads, head_dim)
    keys = keys * lax.rsqrt(jnp.mean(keys * keys, axis=-1, keepdims=True) + epsilon)
    keys = keys * (k_gain * (math.log2(math.e) / math.sqrt(head_dim)))
    own = jnp.concatenate([keys.reshape(image_rows, kv_width), projected[:, kv_width:]], axis=1)
    own = own.astype(jnp.bfloat16)

    sets = [jnp.concatenate([own] + [swap_plane(own, s) for s in range(1, planes)], axis=0)]
    sets.append(swap_lane(sets[0], 1))
    sets.append(swap_lane(sets[0], 2))
    sets.append(swap_lane(sets[2], 1))

    return attend(queries, segment, bias, sets, head_dim)


def solution(mesh):
    placed = (
        P(("groups", "blk"), None),
        P(("groups", "blk"), None),
        P("blk", None),
        P(),
        P(),
        P("groups"),
        P("groups"),
    )
    return jax.shard_map(
        functools.partial(body, mesh.shape["blk"]),
        mesh=mesh,
        in_specs=placed,
        out_specs=P(("groups", "blk"), None),
        check_vma=False,
    )
```
